32 devices in a mesh: pole: 4 (over x, core), row: 4 (over z), col: 2 (over y).
Axes of the slice: x: 2, y: 2, z: 4, core: 2. Of those that a mesh axis runs over, the one named last changes fastest.
Arguments:
- inverse: bfloat16 [4, 2, 6144, 6144], P('pole', None, 'col', 'row'), may hold values from -0.078125 to 0.078125
- factor: bfloat16 [4, 2, 6144, 512], P('pole', None, ('row', 'col')), may hold values from -6 to 6
- block_mask: int32 [2, 192], P(None, ('row', 'col')), may hold values from 0 to 1
- pole_real: float32 [4], P('pole'), may hold values from -1 to 1
- pole_imaginary: float32 [4], P('pole'), may hold values from -1 to 1
Outputs:
- density: bfloat16 [2, 4, 768, 512], P('col', 'row', 'pole')
The draws below stay inside these ranges and needn't reach their ends.
All inputs are finite; a program needn't handle non-finite values.
Results may differ from the reference program's by a relative error of at most 0.0012.
Values may be sent and summed in bfloat16 or wider, within the bound.
A program may use at most 64 MiB of HBM per device.

```python
import jax
import jax.numpy as jnp
from jax import lax

NA = 6144
W = 256
S = 2
BLK = 32
SW = 512
POLES = 4
ROWS_CR = 768
N_ROW = 4
N_COL = 2


def with_ends(result, key, low, high):
    longest = result.shape.index(max(result.shape))
    spots = []
    for shift in (0, 1):
        where = [jax.random.randint(jax.random.fold_in(key, axis), (), 0, length) for axis, length in enumerate(result.shape)]
        where[longest] = (where[longest] + shift) % result.shape[longest]
        spots.append(tuple(where))
    return result.at[spots[0]].set(low).at[spots[1]].set(high)


def block_scale(own_key, extent, shards, smallest, largest):
    gain, own = 1.0, jax.random.fold_in(own_key, 6)
    for dim, parts in shards:
        draws = jnp.exp(jax.random.uniform(jax.random.fold_in(own, dim), (parts,), jnp.float32, smallest / len(shards), largest / len(shards)))
        gain = gain * jnp.repeat(draws, extent[dim] // parts).reshape([-1 if axis == dim else 1 for axis in range(len(extent))])
    return gain


def normal_values(rng, extent, deviation, bound, split=(), kind=jnp.bfloat16):
    drawn = deviation * jax.random.normal(rng, extent, jnp.float32)
    if split:
        drawn = drawn * block_scale(rng, extent, split, -0.22, 0.18)
    return jnp.clip(drawn, -bound, bound).astype(kind)


def setup_inputs(seed: int = 0) -> dict:
    seeds = jax.random.split(jax.random.key(seed), 6)
    return {
        "inverse": normal_values(seeds[0], (POLES, 2, NA, NA), NA ** -0.5, 0.078125, ((0, 4), (2, 2), (3, 4))),
        "factor": normal_values(seeds[1], (POLES, 2, NA, SW), 1.0, 6.0, ((0, 4), (2, 8))),
        "block_mask": with_ends(jax.random.randint(seeds[2], (S, NA // BLK), 0, 2), jax.random.fold_in(seeds[2], 1), 0, 1).astype(jnp.int32),
        "pole_real": jnp.clip(jax.random.uniform(seeds[3], (POLES,), jnp.float32, -1.0, 1.0) * block_scale(seeds[3], (POLES,), ((0, 4),), -0.4, 0.0), -1.0, 1.0),
        "pole_imaginary": jnp.clip(jax.random.uniform(seeds[4], (POLES,), jnp.float32, -1.0, 1.0) * block_scale(seeds[4], (POLES,), ((0, 4),), -0.4, 0.0), -1.0, 1.0),
    }


def pole_term(inverse_pair, factor_pair, column_mask, weight_real, weight_imaginary):
    inverse_real = inverse_pair[0]
    inverse_imaginary = inverse_pair[1]
    masked_real = factor_pair[0] * column_mask
    masked_imaginary = factor_pair[1] * column_mask
    product_real = jnp.dot(inverse_real, masked_real, preferred_element_type=jnp.float32) - jnp.dot(inverse_imaginary, masked_imaginary, preferred_element_type=jnp.float32)
    product_imaginary = jnp.dot(inverse_real, masked_imaginary, preferred_element_type=jnp.float32) + jnp.dot(inverse_imaginary, masked_real, preferred_element_type=jnp.float32)
    return weight_real * product_real - weight_imaginary * product_imaginary


def reference(inverse, factor, block_mask, pole_real, pole_imaginary):
    row_mask = jnp.repeat(block_mask.T, BLK, axis=0)
    column_mask = jnp.repeat(row_mask, W, axis=1).astype(jnp.bfloat16)

    def accumulate(position, running):
        return running + pole_term(inverse[position], factor[position], column_mask, pole_real[position], pole_imaginary[position])

    density = lax.fori_loop(0, POLES, accumulate, jnp.zeros((NA, SW), jnp.float32))
    return density.reshape(N_COL, N_ROW, ROWS_CR, SW).astype(jnp.bfloat16)
```

```python
import functools

import jax
import jax.numpy as jnp
from jax import lax
from jax.experimental import pallas as pl
from jax.experimental.pallas import tpu as pltpu
from jax.sharding import PartitionSpec as P

W = 256
BLK = 32
LANES = 128
MESH = pl.DeviceIdType.MESH


def plain(inverse, factor, block_mask, pole_real, pole_imaginary):
    row_mask = jnp.repeat(block_mask.T, BLK, axis=0)
    column_mask = jnp.repeat(row_mask, W, axis=1).astype(jnp.bfloat16)
    masked = factor[0] * column_mask[None]
    inverse_real = inverse[0, 0]
    inverse_imaginary = inverse[0, 1]
    height = inverse_real.shape[0]
    columns_all = masked.shape[2]
    piece = lax.all_gather(masked, "col", axis=1, tiled=True)
    running_real = jnp.dot(inverse_real, piece[0], preferred_element_type=jnp.float32) - jnp.dot(
        inverse_imaginary, piece[1], preferred_element_type=jnp.float32
    )
    running_imaginary = jnp.dot(
        inverse_real, piece[1], preferred_element_type=jnp.float32
    ) + jnp.dot(inverse_imaginary, piece[0], preferred_element_type=jnp.float32)
    weight_real = pole_real[0]
    weight_imaginary = pole_imaginary[0]
    weighted = weight_real * running_real - weight_imaginary * running_imaginary
    row_count = lax.axis_size("row")
    pole_count = lax.axis_size("pole")
    owned = height // (row_count * pole_count)
    reordered = (
        weighted.reshape(row_count, pole_count, owned, columns_all)
        .transpose(1, 0, 2, 3)
        .reshape(height, columns_all)
    )
    density = lax.psum_scatter(reordered, ("pole", "row"), scatter_dimension=0, tiled=True)
    return density.reshape(1, 1, density.shape[0], columns_all).astype(jnp.bfloat16)


def kernel(
    rows_n,
    real_ref,
    imaginary_ref,
    mask_ref,
    factor_ref,
    inverse_ref,
    out_ref,
    a,
    own_f,
    far_f,
    far_mask,
    mask_wide,
    rhs,
    part,
    core_in,
    x_out,
    x_in,
    z_out,
    z_in,
    load_sem,
    own_sem,
    y_send,
    y_recv,
    m_send,
    m_recv,
    c_send,
    c_recv,
    x_send,
    x_recv,
    z_send,
    z_recv,
):
    p = lax.axis_index("pole")
    z = lax.axis_index("row")
    y = lax.axis_index("col")
    core = lax.rem(p, 2)
    x = p // 2
    sibling = {"pole": x * 2 + 1 - core}
    across = {"pole": (1 - x) * 2 + core}
    beside = {"col": 1 - y}
    depth = factor_ref.shape[2]
    chunks = far_f.shape[0]
    owned = out_ref.shape[2]
    pair = 2 * owned
    group = 4 * owned
    supers, blocks = mask_ref.shape
    per_super = chunks // supers
    steps = 2 * rows_n

    barrier = pltpu.get_barrier_semaphore()
    pl.semaphore_signal(barrier, inc=1, device_id=sibling, device_id_type=MESH)
    pl.semaphore_signal(barrier, inc=1, device_id=across, device_id_type=MESH)
    pl.semaphore_signal(barrier, inc=1, device_id=beside, device_id_type=MESH)
    for d in range(1, rows_n):
        pl.semaphore_signal(
            barrier, inc=1, device_id={"row": lax.rem(z + d, rows_n)}, device_id_type=MESH
        )

    def row_of(j):
        return lax.rem(z + 1 + lax.rem(j, rows_n), rows_n)

    def half_of(j):
        far = j < rows_n
        return jnp.where(far, 1 - x, x)

    def load(j):
        rows = pl.ds(pl.multiple_of(row_of(j) * group + half_of(j) * pair, pair), pair)
        return pltpu.make_async_copy(
            inverse_ref.at[0, :, rows, :], a.at[:, rows, :], load_sem.at[j]
        )

    def own_copy(n):
        return pltpu.make_async_copy(
            factor_ref.at[0, :, :, pl.ds(n * LANES, LANES)], own_f.at[n], own_sem.at[n]
        )

    def gather(n):
        return pltpu.make_async_remote_copy(
            src_ref=factor_ref.at[0, :, :, pl.ds(n * LANES, LANES)],
            dst_ref=far_f.at[n],
            send_sem=y_send.at[n],
            recv_sem=y_recv.at[n],
            device_id=beside,
            device_id_type=MESH,
        )

    masks = pltpu.make_async_remote_copy(
        src_ref=mask_ref,
        dst_ref=far_mask,
        send_sem=m_send,
        recv_sem=m_recv,
        device_id=beside,
        device_id_type=MESH,
    )

    def core_copy(n, j):
        return pltpu.make_async_remote_copy(
            src_ref=part.at[n, row_of(j), half_of(j), 1 - core],
            dst_ref=core_in.at[n, j],
            send_sem=c_send.at[n, j],
            recv_sem=c_recv.at[n, j],
            device_id=sibling,
            device_id_type=MESH,
        )

    def x_copy(n, j):
        return pltpu.make_async_remote_copy(
            src_ref=x_out.at[n, j],
            dst_ref=x_in.at[n, j],
            send_sem=x_send.at[n, j],
            recv_sem=x_recv.at[n, j],
            device_id=across,
            device_id_type=MESH,
        )

    def z_copy(n, d):
        return pltpu.make_async_remote_copy(
            src_ref=z_out.at[n, d],
            dst_ref=z_in.at[n, d],
            send_sem=z_send.at[n, d],
            recv_sem=z_recv.at[n, d],
            device_id={"row": lax.rem(z + 1 + d, rows_n)},
            device_id_type=MESH,
        )

    for n in range(chunks):
        own_copy(n).start()
    pl.semaphore_wait(barrier, 3 + rows_n - 1)
    masks.start()
    for n in range(chunks):
        gather(n).start()
    for j in range(steps):
        load(j).start()

    def widen(half, ref):
        values = ref[...].astype(jnp.float32)
        row = lax.broadcasted_iota(jnp.int32, (depth, blocks), 0)
        block = lax.broadcasted_iota(jnp.int32, (depth, blocks), 1)
        low = block * (depth // blocks)
        inside = jnp.logical_and(row >= low, row < low + depth // blocks)
        for s in range(supers):
            spread = jnp.where(inside, values[s : s + 1, :], 0.0)
            column = jnp.sum(spread, axis=1, keepdims=True)
            mask_wide[half, s] = jnp.broadcast_to(column, (depth, LANES)).astype(jnp.bfloat16)

    widen(0, mask_ref)
    masks.wait_recv()
    widen(1, far_mask)
    own_rows = pl.ds(pl.multiple_of(y * depth, depth), depth)
    far_rows = pl.ds(pl.multiple_of((1 - y) * depth, depth), depth)
    for n in range(chunks):
        own_copy(n).wait()
        for part_index in range(2):
            rhs[n, own_rows, part_index * LANES : (part_index + 1) * LANES] = (
                own_f[n, part_index] * mask_wide[0, n // per_super]
            )
    weight_real = real_ref[0]
    weight_imaginary = imaginary_ref[0]

    def send_x(n, j):
        core_copy(n, j).wait_recv()
        x_out[n, j] = part[n, row_of(j), half_of(j), core] + core_in[n, j]
        x_copy(n, j).start()

    def compute(n):
        def body(j, carry):
            if n == 0:
                load(j).wait()
            r = row_of(j)
            h = half_of(j)
            rows = pl.ds(pl.multiple_of(r * group + h * pair, pair), pair)
            by_real = jnp.dot(a[0, rows, :], rhs[n], preferred_element_type=jnp.float32)
            by_imaginary = jnp.dot(a[1, rows, :], rhs[n], preferred_element_type=jnp.float32)
            real = by_real[:, :LANES] - by_imaginary[:, LANES:]
            imaginary = by_real[:, LANES:] + by_imaginary[:, :LANES]
            weighted = weight_real * real - weight_imaginary * imaginary
            part[n, r, h] = weighted.reshape(2, owned, LANES)
            core_copy(n, j).start()

            @pl.when(jnp.logical_and(j >= 1, j <= rows_n))
            def _():
                send_x(n, j - 1)

            return carry

        lax.fori_loop(0, steps, body, 0)

    def send_z(n):
        def body(d, carry):
            j = d + rows_n
            core_copy(n, j).wait_recv()
            x_copy(n, d).wait_recv()
            z_out[n, d] = part[n, row_of(d), x, core] + core_in[n, j] + x_in[n, d]

            @pl.when(d < rows_n - 1)
            def _():
                z_copy(n, d).start()

            return carry

        lax.fori_loop(0, rows_n, body, 0)

    def finish(n):
        total = z_out[n, rows_n - 1]
        for d in range(rows_n - 1):
            z_copy(n, d).wait_recv()
            total = total + z_in[n, d]
        out_ref[0, 0, :, n * LANES : (n + 1) * LANES] = total.astype(out_ref.dtype)

    for n in range(chunks):
        gather(n).wait_recv()
        for part_index in range(2):
            rhs[n, far_rows, part_index * LANES : (part_index + 1) * LANES] = (
                far_f[n, part_index] * mask_wide[1, n // per_super]
            )
        compute(n)
        if n >= 1:
            send_z(n - 1)
        if n >= 2:
            finish(n - 2)
    send_z(chunks - 1)
    for n in range(max(chunks - 2, 0), chunks):
        finish(n)

    masks.wait_send()
    for n in range(chunks):
        gather(n).wait_send()

        def drain(j, carry):
            core_copy(n, j).wait_send()

            @pl.when(j < rows_n)
            def _():
                x_copy(n, j).wait_send()

            @pl.when(j < rows_n - 1)
            def _():
                z_copy(n, j).wait_send()

            return carry

        lax.fori_loop(0, steps, drain, 0)


def fused(inverse, factor, block_mask, pole_real, pole_imaginary):
    rows_n = lax.axis_size("row")
    height, width = inverse.shape[2:]
    depth, columns_all = factor.shape[2:]
    chunks = columns_all // LANES
    owned = height // (rows_n * 4)
    f32 = jnp.float32
    dma = pltpu.SemaphoreType.DMA
    smem = pl.BlockSpec(memory_space=pltpu.SMEM)
    vmem = pl.BlockSpec(memory_space=pltpu.VMEM)
    anywhere = pl.BlockSpec(memory_space=pl.ANY)
    return pl.pallas_call(
        functools.partial(kernel, rows_n),
        out_shape=jax.ShapeDtypeStruct((1, 1, owned, columns_all), jnp.bfloat16),
        in_specs=[smem, smem, vmem, anywhere, anywhere],
        out_specs=vmem,
        scratch_shapes=[
            pltpu.VMEM((2, height, width), jnp.bfloat16),
            pltpu.VMEM((chunks, 2, depth, LANES), jnp.bfloat16),
            pltpu.VMEM((chunks, 2, depth, LANES), jnp.bfloat16),
            pltpu.VMEM(block_mask.shape, block_mask.dtype),
            pltpu.VMEM((2, block_mask.shape[0], depth, LANES), jnp.bfloat16),
            pltpu.VMEM((chunks, 2 * depth, 2 * LANES), jnp.bfloat16),
            pltpu.VMEM((chunks, rows_n, 2, 2, owned, LANES), f32),
            pltpu.VMEM((chunks, 2 * rows_n, owned, LANES), f32),
            pltpu.VMEM((chunks, rows_n, owned, LANES), f32),
            pltpu.VMEM((chunks, rows_n, owned, LANES), f32),
            pltpu.VMEM((chunks, rows_n, owned, LANES), f32),
            pltpu.VMEM((chunks, rows_n, owned, LANES), f32),
            dma((2 * rows_n,)),
            dma((chunks,)),
            dma((chunks,)),
            dma((chunks,)),
            dma,
            dma,
            dma((chunks, 2 * rows_n)),
            dma((chunks, 2 * rows_n)),
            dma((chunks, rows_n)),
            dma((chunks, rows_n)),
            dma((chunks, rows_n)),
            dma((chunks, rows_n)),
        ],
        compiler_params=pltpu.CompilerParams(
            collective_id=0, has_side_effects=True, vmem_limit_bytes=60 * 1024 * 1024
        ),
    )(pole_real, pole_imaginary, block_mask, factor, inverse)


def solution(mesh):
    sizes = dict(mesh.shape)

    def shards(inverse, factor, block_mask, pole_real, pole_imaginary):
        supers = block_mask.shape[0]
        wide = factor.shape[3] // supers
        small = 2 * inverse.shape[2] * inverse.shape[3] * 2 <= 20 * 1024 * 1024
        fits = sizes["pole"] == 4 and sizes["col"] == 2 and sizes["row"] >= 2
        if fits and small and wide % LANES == 0:
            body = fused
        else:
            body = plain
        return body(inverse, factor, block_mask, pole_real, pole_imaginary)

    return jax.shard_map(
        shards,
        mesh=mesh,
        in_specs=(
            P("pole", None, "col", "row"),
            P("pole", None, ("row", "col"), None),
            P(None, ("row", "col")),
            P("pole"),
            P("pole"),
        ),
        out_specs=P("col", "row", "pole", None),
        check_vma=False,
    )
```

```python
import functools

import jax
import jax.numpy as jnp
from jax import lax
from jax.experimental import pallas as pl
from jax.experimental.pallas import tpu as pltpu
from jax.sharding import PartitionSpec as P

W = 256
BLK = 32
LANES = 128
MESH = pl.DeviceIdType.MESH


def plain(inverse, factor, block_mask, pole_real, pole_imaginary):
    row_mask = jnp.repeat(block_mask.T, BLK, axis=0)
    column_mask = jnp.repeat(row_mask, W, axis=1).astype(jnp.bfloat16)
    masked = factor[0] * column_mask[None]
    inverse_real = inverse[0, 0]
    inverse_imaginary = inverse[0, 1]
    height = inverse_real.shape[0]
    columns_all = masked.shape[2]
    piece = lax.all_gather(masked, "col", axis=1, tiled=True)
    running_real = jnp.dot(inverse_real, piece[0], preferred_element_type=jnp.float32) - jnp.dot(
        inverse_imaginary, piece[1], preferred_element_type=jnp.float32
    )
    running_imaginary = jnp.dot(
        inverse_real, piece[1], preferred_element_type=jnp.float32
    ) + jnp.dot(inverse_imaginary, piece[0], preferred_element_type=jnp.float32)
    weight_real = pole_real[0]
    weight_imaginary = pole_imaginary[0]
    weighted = weight_real * running_real - weight_imaginary * running_imaginary
    row_count = lax.axis_size("row")
    pole_count = lax.axis_size("pole")
    owned = height // (row_count * pole_count)
    reordered = (
        weighted.reshape(row_count, pole_count, owned, columns_all)
        .transpose(1, 0, 2, 3)
        .reshape(height, columns_all)
    )
    density = lax.psum_scatter(reordered, ("pole", "row"), scatter_dimension=0, tiled=True)
    return density.reshape(1, 1, density.shape[0], columns_all).astype(jnp.bfloat16)


def kernel(
    rows_n,
    real_hbm,
    imaginary_hbm,
    mask_hbm,
    factor_ref,
    inverse_ref,
    out_ref,
    a,
    own_f,
    far_f,
    real_ref,
    imaginary_ref,
    mask_ref,
    far_mask,
    mask_wide,
    rhs,
    part,
    core_in,
    x_out,
    x_in,
    z_out,
    z_in,
    load_sem,
    own_sem,
    small_sem,
    y_send,
    y_recv,
    m_send,
    m_recv,
    c_send,
    c_recv,
    x_send,
    x_recv,
    z_send,
    z_recv,
):
    p = lax.axis_index("pole")
    z = lax.axis_index("row")
    y = lax.axis_index("col")
    core = lax.rem(p, 2)
    x = p // 2
    sibling = {"pole": x * 2 + 1 - core}
    across = {"pole": (1 - x) * 2 + core}
    beside = {"col": 1 - y}
    depth = factor_ref.shape[2]
    chunks = far_f.shape[0]
    owned = out_ref.shape[2]
    pair = 2 * owned
    group = 4 * owned
    supers, blocks = mask_ref.shape
    per_super = chunks // supers
    steps = 2 * rows_n

    barrier = pltpu.get_barrier_semaphore()
    pl.semaphore_signal(barrier, inc=1, device_id=sibling, device_id_type=MESH)
    pl.semaphore_signal(barrier, inc=1, device_id=across, device_id_type=MESH)
    pl.semaphore_signal(barrier, inc=1, device_id=beside, device_id_type=MESH)
    for d in range(1, rows_n):
        pl.semaphore_signal(
            barrier, inc=1, device_id={"row": lax.rem(z + d, rows_n)}, device_id_type=MESH
        )

    def partner(j):
        step = rows_n - 1 - j
        if rows_n & (rows_n - 1):
            return lax.rem(z + rows_n - step, rows_n)
        other = 0
        bit = 1
        while bit < rows_n:
            other = other + bit * lax.rem(z // bit + step // bit, 2)
            bit *= 2
        return other

    def row_of(j):
        return partner(lax.rem(j, rows_n))

    def half_of(j):
        far = j < rows_n
        return jnp.where(far, 1 - x, x)

    def load(j):
        rows = pl.ds(pl.multiple_of(row_of(j) * group + half_of(j) * pair, pair), pair)
        return pltpu.make_async_copy(
            inverse_ref.at[0, :, rows, :], a.at[:, rows, :], load_sem.at[j]
        )

    def own_copy(n):
        return pltpu.make_async_copy(
            factor_ref.at[0, :, :, pl.ds(n * LANES, LANES)], own_f.at[n], own_sem.at[n]
        )

    def gather(n):
        return pltpu.make_async_remote_copy(
            src_ref=factor_ref.at[0, :, :, pl.ds(n * LANES, LANES)],
            dst_ref=far_f.at[n],
            send_sem=y_send.at[n],
            recv_sem=y_recv.at[n],
            device_id=beside,
            device_id_type=MESH,
        )

    masks = pltpu.make_async_remote_copy(
        src_ref=mask_hbm,
        dst_ref=far_mask,
        send_sem=m_send,
        recv_sem=m_recv,
        device_id=beside,
        device_id_type=MESH,
    )

    def core_copy(n, j):
        return pltpu.make_async_remote_copy(
            src_ref=part.at[n, row_of(j), half_of(j), 1 - core],
            dst_ref=core_in.at[n, j],
            send_sem=c_send.at[n, j],
            recv_sem=c_recv.at[n, j],
            device_id=sibling,
            device_id_type=MESH,
        )

    def x_copy(n, j):
        return pltpu.make_async_remote_copy(
            src_ref=x_out.at[n, j],
            dst_ref=x_in.at[n, j],
            send_sem=x_send.at[n, j],
            recv_sem=x_recv.at[n, j],
            device_id=across,
            device_id_type=MESH,
        )

    def z_copy(n, d):
        return pltpu.make_async_remote_copy(
            src_ref=z_out.at[n, d],
            dst_ref=z_in.at[n, d],
            send_sem=z_send.at[n, d],
            recv_sem=z_recv.at[n, d],
            device_id={"row": partner(d)},
            device_id_type=MESH,
        )

    small = [
        pltpu.make_async_copy(source, target, small_sem.at[i])
        for i, (source, target) in enumerate(
            ((mask_hbm, mask_ref), (real_hbm, real_ref), (imaginary_hbm, imaginary_ref))
        )
    ]
    for copy in small:
        copy.start()
    for n in range(chunks):
        own_copy(n).start()
    pl.semaphore_wait(barrier, 3 + rows_n - 1)
    masks.start()
    for n in range(chunks):
        gather(n).start()
    for j in range(steps):
        load(j).start()

    def widen(half, ref):
        values = ref[...].astype(jnp.float32)
        row = lax.broadcasted_iota(jnp.int32, (depth, blocks), 0)
        block = lax.broadcasted_iota(jnp.int32, (depth, blocks), 1)
        low = block * (depth // blocks)
        inside = jnp.logical_and(row >= low, row < low + depth // blocks)
        for s in range(supers):
            spread = jnp.where(inside, values[s : s + 1, :], 0.0)
            column = jnp.sum(spread, axis=1, keepdims=True)
            mask_wide[half, s] = jnp.broadcast_to(column, (depth, LANES)).astype(jnp.bfloat16)

    for copy in small:
        copy.wait()
    widen(0, mask_ref)
    masks.wait_recv()
    widen(1, far_mask)
    own_rows = pl.ds(pl.multiple_of(y * depth, depth), depth)
    far_rows = pl.ds(pl.multiple_of((1 - y) * depth, depth), depth)
    for n in range(chunks):
        own_copy(n).wait()
        for part_index in range(2):
            rhs[n, own_rows, part_index * LANES : (part_index + 1) * LANES] = (
                own_f[n, part_index] * mask_wide[0, n // per_super]
            )
    weight_real = real_ref[0]
    weight_imaginary = imaginary_ref[0]

    def send_x(n, j):
        core_copy(n, j).wait_recv()
        x_out[n, j] = part[n, row_of(j), half_of(j), core] + core_in[n, j]
        x_copy(n, j).start()

    def compute(n):
        def body(j, carry):
            if n == 0:
                load(j).wait()
            r = row_of(j)
            h = half_of(j)
            rows = pl.ds(pl.multiple_of(r * group + h * pair, pair), pair)
            by_real = jnp.dot(a[0, rows, :], rhs[n], preferred_element_type=jnp.float32)
            by_imaginary = jnp.dot(a[1, rows, :], rhs[n], preferred_element_type=jnp.float32)
            real = by_real[:, :LANES] - by_imaginary[:, LANES:]
            imaginary = by_real[:, LANES:] + by_imaginary[:, :LANES]
            weighted = weight_real * real - weight_imaginary * imaginary
            part[n, r, h] = weighted.reshape(2, owned, LANES)
            core_copy(n, j).start()

            @pl.when(jnp.logical_and(j >= 1, j <= rows_n))
            def _():
                send_x(n, j - 1)

            if n >= 1:

                @pl.when(jnp.logical_and(j >= 1, j <= rows_n - early))
                def _():
                    send_z(n - 1, early + j - 1)

            return carry

        lax.fori_loop(0, steps, body, 0)

    early = rows_n // 2

    def send_z(n, d):
        j = d + rows_n
        core_copy(n, j).wait_recv()
        x_copy(n, d).wait_recv()
        z_out[n, d] = part[n, row_of(d), x, core] + core_in[n, j] + x_in[n, d]

        @pl.when(d < rows_n - 1)
        def _():
            z_copy(n, d).start()

    def send_z_range(n, low, high):
        def body(d, carry):
            send_z(n, d)
            return carry

        lax.fori_loop(low, high, body, 0)

    def finish(n):
        total = z_out[n, rows_n - 1]
        for d in range(rows_n - 1):
            z_copy(n, d).wait_recv()
            total = total + z_in[n, d]
        out_ref[0, 0, :, n * LANES : (n + 1) * LANES] = total.astype(out_ref.dtype)

    for n in range(chunks):
        if n >= 1:
            send_z_range(n - 1, 0, early)
        gather(n).wait_recv()
        for part_index in range(2):
            rhs[n, far_rows, part_index * LANES : (part_index + 1) * LANES] = (
                far_f[n, part_index] * mask_wide[1, n // per_super]
            )
        compute(n)
        if n >= 2:
            finish(n - 2)
    send_z_range(chunks - 1, 0, early)
    if chunks >= 2:
        finish(chunks - 2)
    send_z_range(chunks - 1, early, rows_n)
    finish(chunks - 1)

    masks.wait_send()
    for n in range(chunks):
        gather(n).wait_send()

        def drain(j, carry):
            core_copy(n, j).wait_send()

            @pl.when(j < rows_n)
            def _():
                x_copy(n, j).wait_send()

            @pl.when(j < rows_n - 1)
            def _():
                z_copy(n, j).wait_send()

            return carry

        lax.fori_loop(0, steps, drain, 0)


def fused(inverse, factor, block_mask, pole_real, pole_imaginary):
    rows_n = lax.axis_size("row")
    height, width = inverse.shape[2:]
    depth, columns_all = factor.shape[2:]
    chunks = columns_all // LANES
    owned = height // (rows_n * 4)
    f32 = jnp.float32
    dma = pltpu.SemaphoreType.DMA
    vmem = pl.BlockSpec(memory_space=pltpu.VMEM)
    anywhere = pl.BlockSpec(memory_space=pl.ANY)
    return pl.pallas_call(
        functools.partial(kernel, rows_n),
        out_shape=jax.ShapeDtypeStruct((1, 1, owned, columns_all), jnp.bfloat16),
        in_specs=[anywhere] * 5,
        out_specs=vmem,
        scratch_shapes=[
            pltpu.VMEM((2, height, width), jnp.bfloat16),
            pltpu.VMEM((chunks, 2, depth, LANES), jnp.bfloat16),
            pltpu.VMEM((chunks, 2, depth, LANES), jnp.bfloat16),
            pltpu.SMEM(pole_real.shape, f32),
            pltpu.SMEM(pole_imaginary.shape, f32),
            pltpu.VMEM(block_mask.shape, block_mask.dtype),
            pltpu.VMEM(block_mask.shape, block_mask.dtype),
            pltpu.VMEM((2, block_mask.shape[0], depth, LANES), jnp.bfloat16),
            pltpu.VMEM((chunks, 2 * depth, 2 * LANES), jnp.bfloat16),
            pltpu.VMEM((chunks, rows_n, 2, 2, owned, LANES), f32),
            pltpu.VMEM((chunks, 2 * rows_n, owned, LANES), f32),
            pltpu.VMEM((chunks, rows_n, owned, LANES), f32),
            pltpu.VMEM((chunks, rows_n, owned, LANES), f32),
            pltpu.VMEM((chunks, rows_n, owned, LANES), f32),
            pltpu.VMEM((chunks, rows_n, owned, LANES), f32),
            dma((2 * rows_n,)),
            dma((chunks,)),
            dma((3,)),
            dma((chunks,)),
            dma((chunks,)),
            dma,
            dma,
            dma((chunks, 2 * rows_n)),
            dma((chunks, 2 * rows_n)),
            dma((chunks, rows_n)),
            dma((chunks, rows_n)),
            dma((chunks, rows_n)),
            dma((chunks, rows_n)),
        ],
        compiler_params=pltpu.CompilerParams(
            collective_id=0, has_side_effects=True, vmem_limit_bytes=60 * 1024 * 1024
        ),
    )(pole_real, pole_imaginary, block_mask, factor, inverse)


def solution(mesh):
    sizes = dict(mesh.shape)

    def shards(inverse, factor, block_mask, pole_real, pole_imaginary):
        supers = block_mask.shape[0]
        wide = factor.shape[3] // supers
        small = 2 * inverse.shape[2] * inverse.shape[3] * 2 <= 20 * 1024 * 1024
        fits = sizes["pole"] == 4 and sizes["col"] == 2 and sizes["row"] >= 2
        if fits and small and wide % LANES == 0:
            body = fused
        else:
            body = plain
        return body(inverse, factor, block_mask, pole_real, pole_imaginary)

    return jax.shard_map(
        shards,
        mesh=mesh,
        in_specs=(
            P("pole", None, "col", "row"),
            P("pole", None, ("row", "col"), None),
            P(None, ("row", "col")),
            P("pole"),
            P("pole"),
        ),
        out_specs=P("col", "row", "pole", None),
        check_vma=False,
    )
```
